128 devices in a mesh: band: 4 (over y), tile: 32 (over x, z, core).
Axes of the slice: x: 4, y: 4, z: 4, core: 2. Of those that a mesh axis runs over, the one named last changes fastest.
Arguments:
- winds: float32 [2, 8, 48, 256, 720], P(None, None, 'band', 'tile'), may hold values from -8 to 8
- basis: bfloat16 [24, 48, 2, 256, 720], P(None, 'band', None, 'tile'), may hold values from -48 to 48
- ground: int32 [256, 720], P('tile'), may hold values from 24 to 48
Outputs:
- new_basis: float32 [24, 48, 2, 256, 720], P(None, 'band', None, 'tile')
The draws below stay inside these ranges and needn't reach their ends.
All inputs are finite; a program needn't handle non-finite values.
Results may differ from the reference program's by a relative error of at most 0.0015.
Values sent between devices are 32-bit elements; how exact they have to be, the bound alone decides.
A program may use at most 128 MiB of HBM per device.

```python
import math
import jax
import jax.numpy as jnp
from jax import lax

K = 24
SNAP = 8
ITERS = 4
LAT = 720
LEVELS = 48
NLON = 256
COLS = 32


def lat_diff_drawn(field):
    ext = jnp.pad(field, [(0, 0)] * (field.ndim - 1) + [(2, 2)])
    return (8.0 * (ext[..., 3:-1] - ext[..., 1:-3]) - (ext[..., 4:] - ext[..., :-4])) / 12.0


def lon_diff_drawn(field):
    return (8.0 * (jnp.roll(field, -1, -2) - jnp.roll(field, 1, -2)) - (jnp.roll(field, -2, -2) - jnp.roll(field, 2, -2))) / 12.0


def shared_modes(key):
    mode_key = jax.random.fold_in(key, 101)
    shape = (6, 2, LEVELS, NLON, LAT)
    return jax.random.truncated_normal(mode_key, -6.0, 6.0, shape, jnp.float32)


def mode_fields(modes):
    cosine = jnp.cos((jnp.arange(LAT, dtype=jnp.float32) + 0.5) * (jnp.pi / LAT) - jnp.pi / 2)
    spread = 0.9 * (2.0 / math.pi * math.log(4.0 * LAT / math.pi) + 0.64)
    east_wind = modes[:, 0]
    north_wind = modes[:, 1]
    vorticity = (lon_diff_drawn(north_wind) - lat_diff_drawn(east_wind * cosine)) / cosine
    divergence = (lon_diff_drawn(east_wind) + lat_diff_drawn(north_wind * cosine)) / cosine
    return jnp.stack([vorticity, divergence], axis=2) * (jnp.sqrt(cosine) / math.sqrt(spread))


def draw_winds(key, part):
    modes = shared_modes(key)
    noise_key = jax.random.fold_in(key, 202)
    loading_key = jax.random.fold_in(key, 303)
    shape = (2, SNAP, LEVELS, NLON, LAT)
    winds = 0.8 * jax.random.truncated_normal(noise_key, -6.0, 6.0, shape, jnp.float32)
    loading = 0.5 * jax.random.normal(loading_key, (SNAP, 6), jnp.float32)
    for mode_id in range(6):
        winds = winds + loading[:, mode_id][None, :, None, None, None] * modes[mode_id][:, None]
    return jnp.clip(winds, -8.0, 8.0)


def draw_basis(key, part):
    fields = mode_fields(shared_modes(key))
    noise_key = jax.random.fold_in(key, 404)
    mixing_key = jax.random.fold_in(key, 505)
    shape = (K, LEVELS, 2, NLON, LAT)
    steps_k = jnp.arange(K, dtype=jnp.float32)
    basis = jax.random.truncated_normal(noise_key, -6.0, 6.0, shape, jnp.float32)
    mixing = 0.4 * jax.random.normal(mixing_key, (K, 6), jnp.float32)
    scales = 2.0 * jnp.power(0.97, steps_k)
    for mode_id in range(6):
        basis = basis + mixing[:, mode_id][:, None, None, None, None] * fields[mode_id][None]
    return jnp.clip(basis * scales[:, None, None, None, None], -48.0, 48.0).astype(jnp.bfloat16)


def touch_ends(array, own_key, least, top_value):
    index_at = [jax.random.randint(jax.random.fold_in(own_key, axis), (), 0, length) for axis, length in enumerate(array.shape)]
    widest = array.shape.index(max(array.shape))
    next_to = index_at[:widest] + [(index_at[widest] + 1) % array.shape[widest]] + index_at[widest + 1:]
    return array.at[tuple(index_at)].set(least).at[tuple(next_to)].set(top_value)


def setup_inputs(seed: int = 0) -> dict:
    streams_of = jax.random.split(jax.random.key(seed), 4)
    return {
        "winds": draw_winds(jax.random.fold_in(streams_of[3], 71), 0),
        "basis": draw_basis(jax.random.fold_in(streams_of[3], 71), 0),
        "ground": touch_ends(jax.random.randint(streams_of[2], (NLON, LAT), LEVELS // 2, LEVELS + 1), jax.random.fold_in(streams_of[2], 1), LEVELS // 2, LEVELS).astype(jnp.int32),
    }


HIGH = lax.Precision.HIGHEST

def lat_diff(field):
    ext = jnp.pad(field, [(0, 0)] * (field.ndim - 1) + [(2, 2)])
    return (8.0 * (ext[..., 3:-1] - ext[..., 1:-3]) - (ext[..., 4:] - ext[..., :-4])) / 12.0

def lon_diff(field):
    return (8.0 * (jnp.roll(field, -1, -2) - jnp.roll(field, 1, -2)) - (jnp.roll(field, -2, -2) - jnp.roll(field, 2, -2))) / 12.0

def orthonormal(block):

    def one_column(col_id, ortho):
        column = lax.dynamic_index_in_dim(block, col_id, 1, keepdims=False)
        for repeat in range(2):
            column = column - jnp.dot(ortho, jnp.dot(column, ortho, precision=HIGH), precision=HIGH)
        column = column / jnp.sqrt(jnp.dot(column, column, precision=HIGH))
        return lax.dynamic_update_index_in_dim(ortho, column, col_id, 1)
    return lax.fori_loop(0, block.shape[1], one_column, jnp.zeros_like(block))

def reference(winds, basis, ground):
    cosine = jnp.cos((jnp.arange(LAT, dtype=jnp.float32) + 0.5) * (jnp.pi / LAT) - jnp.pi / 2)
    weight = jnp.sqrt(cosine)

    def stacked_level(level_id):
        wind_level = lax.dynamic_index_in_dim(winds, level_id, 2, keepdims=False)
        basis_level = lax.dynamic_index_in_dim(basis, level_id, 1, keepdims=False)
        east_wind, north_wind = (wind_level[0], wind_level[1])
        vorticity = (lon_diff(north_wind) - lat_diff(east_wind * cosine)) / cosine
        divergence = (lon_diff(east_wind) + lat_diff(north_wind * cosine)) / cosine
        inside_air = (level_id < ground).astype(jnp.float32)
        snapshot_cols = (jnp.stack([vorticity, divergence], axis=1) * (weight * inside_air)).astype(jnp.bfloat16)
        stacked = jnp.concatenate([basis_level, snapshot_cols], axis=0)
        return stacked.reshape(stacked.shape[0], -1)
    level_ids = jnp.arange(LEVELS, dtype=jnp.int32)

    def add_level(total, level_id):
        stacked = stacked_level(level_id)
        return (total + jnp.dot(stacked, stacked.T, preferred_element_type=jnp.float32), None)
    gram, _ = lax.scan(add_level, jnp.zeros((COLS, COLS), jnp.float32), level_ids)
    frame = jnp.eye(COLS, K, dtype=jnp.float32)
    for sweep in range(ITERS):
        frame = orthonormal(jnp.dot(gram, frame, precision=HIGH))

    def project(level_id):
        stacked = stacked_level(level_id).astype(jnp.float32)
        return jnp.dot(frame.T, stacked, precision=HIGH).reshape(K, 2, NLON, LAT)
    result = lax.map(project, level_ids)
    return jnp.transpose(result, (1, 0, 2, 3, 4))
```

```python
import functools

import jax
import jax.numpy as jnp
import numpy as np
from jax import lax
from jax.experimental import pallas as pl
from jax.experimental.pallas import tpu as pltpu
from jax.sharding import PartitionSpec as P

ITERS = 4
MESH = pl.DeviceIdType.MESH
HIGH = lax.Precision.HIGHEST
LANES = 128
ROWS = 8


def padded(x, width):
    return jnp.concatenate([x, jnp.zeros((x.shape[0], width - x.shape[1]), x.dtype)], axis=1)


def turned(x, shift, axis):
    shift %= x.shape[axis]
    return x if shift == 0 else pltpu.roll(x, shift, axis)


def gather_kernel(
    bands, tiles, rank, snaps,
    winds, basis, ground, cosine, factor, pick,
    stacked, gram,
    wind, old, cols, send, recv, keep, total, near, far, across,
    wind_sem, old_sem, out_sem, send_sem, recv_sem, near_send, near_recv, far_send, far_recv, across_send, across_recv,
):
    levels = winds.shape[2]
    lat = winds.shape[4]
    width = cols.shape[2]
    near_n, far_n = near.shape[0], far.shape[0]
    quads = snaps // 4
    band = lax.axis_index("band")
    tile = lax.axis_index("tile")
    right = lax.rem(tile + 1, tiles)
    left = lax.rem(tile + tiles - 1, tiles)

    def wind_copy(level):
        return pltpu.make_async_copy(winds.at[:, :, level], wind.at[:, :, level], wind_sem.at[level])

    def old_copy(level):
        return pltpu.make_async_copy(basis.at[:, level], old.at[:, level], old_sem.at[level])

    def out_copy(level):
        return pltpu.make_async_copy(
            cols.at[pl.ds(2 * level, 2)], stacked.at[pl.ds(2 * level, 2)], out_sem.at[level]
        )

    def edge_copy(way, level):
        return pltpu.make_async_remote_copy(
            src_ref=send.at[way, level],
            dst_ref=recv.at[way, level],
            send_sem=send_sem.at[way, level],
            recv_sem=recv_sem.at[way, level],
            device_id=(band, right if way == 0 else left),
            device_id_type=MESH,
        )

    @pl.loop(0, levels)
    def _(level):
        wind_copy(level).start()

    @pl.loop(0, levels)
    def _(level):
        old_copy(level).start()

    near_at = lax.rem(tile, near_n)
    far_at = lax.div(tile, near_n)
    near_peers = [(band, far_at * near_n + lax.rem(near_at + d, near_n)) for d in range(1, near_n)]
    far_peers = [(band, lax.rem(tile + d * near_n, tiles)) for d in range(1, far_n)]
    band_peers = [(lax.rem(band + d, bands), tile) for d in range(1, bands)]
    barrier = pltpu.get_barrier_semaphore()
    greeted = [(band, left), (band, right)] + near_peers + far_peers + band_peers
    for peer in greeted:
        pl.semaphore_signal(barrier, inc=1, device_id=peer, device_id_type=MESH)

    row = lax.broadcasted_iota(jnp.int32, (ROWS, 1), 0)

    def pack(level):
        for field in range(2):
            for quad in range(quads):
                at = [turned(wind[field, 4 * quad + j, level], 2 * j, 0) for j in range(4)]
                slot = pl.ds((field * quads + quad) * ROWS, ROWS)
                send[1, level, slot, :] = jnp.where(
                    row < 2, at[0], jnp.where(row < 4, at[1], jnp.where(row < 6, at[2], at[3]))
                )
                send[0, level, slot, :] = jnp.where(
                    row < 2, at[1], jnp.where(row < 4, at[2], jnp.where(row < 6, at[3], at[0]))
                )

    wind_copy(0).wait()
    pack(0)
    pl.semaphore_wait(barrier, len(greeted))

    @pl.loop(1, levels)
    def _(level):
        wind_copy(level).wait()
        pack(level)
        edge_copy(0, level - 1).start()
        edge_copy(1, level - 1).start()

    keep[...] = padded(ground[...], width)
    total[...] = jnp.zeros_like(total)
    edge_copy(0, levels - 1).start()
    edge_copy(1, levels - 1).start()

    @pl.loop(0, levels)
    def _(level):
        old_copy(level).wait()
        for field in range(2):
            for pair in range(rank // 2):
                two = old[pl.ds(2 * pair, 2), level, field].astype(jnp.float32)
                two = two.reshape(2 * ROWS, lat)
                cols[2 * level + field, pl.ds(2 * ROWS * pair, 2 * ROWS), :] = padded(two, width).astype(jnp.bfloat16)

    def along_lon(x, edge, j):
        after = [row == 2 * j, (row == 2 * j) | (row == 2 * j + 1)]
        edge = turned(jnp.where(after[1], edge[0], edge[1]), -2 * j, 0)
        near_diff = turned(jnp.where(row == 0, edge, x), -1, 0) - turned(jnp.where(row == 7, edge, x), 1, 0)
        far_diff = turned(jnp.where(row < 2, edge, x), -2, 0) - turned(jnp.where(row >= 6, edge, x), 2, 0)
        return 8.0 * near_diff - far_diff

    def along_lat(x):
        near_diff = turned(x, -1, 1) - turned(x, 1, 1)
        far_diff = turned(x, -2, 1) - turned(x, 2, 1)
        return 8.0 * near_diff - far_diff

    def product(level):
        out = None
        for field in range(2):
            m = cols[2 * level + field]
            part = lax.dot_general(m, m, (((1,), (1,)), ((), ())), preferred_element_type=jnp.float32)
            out = part if out is None else out + part
        total[...] += out

    def snapshots(level):
        edge_copy(0, level).wait_recv()
        edge_copy(1, level).wait_recv()
        cos = cosine[...]
        scale = jnp.where(band * levels + level < keep[...], factor[...], 0.0)
        for pair in range(snaps // 2):
            found = [[], []]
            for snap in (2 * pair, 2 * pair + 1):
                quad, j = divmod(snap, 4)
                east, north = (padded(wind[field, snap, level], width) for field in range(2))
                edges = []
                for field in range(2):
                    slot = pl.ds((field * quads + quad) * ROWS, ROWS)
                    edges.append([padded(recv[way, level, slot, :], width) for way in (1, 0)])
                found[0].append((along_lon(north, edges[1], j) - along_lat(east * cos)) * scale)
                found[1].append((along_lon(east, edges[0], j) + along_lat(north * cos)) * scale)
            for field in range(2):
                both = jnp.concatenate(found[field], axis=0).astype(jnp.bfloat16)
                cols[2 * level + field, pl.ds((rank + 2 * pair) * ROWS, 2 * ROWS), :] = both

    snapshots(0)

    @pl.loop(1, levels)
    def _(level):
        product(level - 1)
        snapshots(level)
        out_copy(level - 1).start()

    product(levels - 1)
    out_copy(levels - 1).start()

    side = total.shape[0]
    same = (
        lax.rem(lax.broadcasted_iota(jnp.int32, (ROWS, side), 1), ROWS)
        == lax.broadcasted_iota(jnp.int32, (ROWS, side), 0)
    )
    blocks = jnp.where(same[None], total[...].reshape(side // ROWS, ROWS, side), 0.0).sum(axis=1)
    wide = jnp.dot(blocks, pick[...], precision=HIGH, preferred_element_type=jnp.float32)
    group = lax.div(lax.broadcasted_iota(jnp.int32, (ROWS, LANES), 1), side // ROWS)
    part = wide[0:ROWS]
    for q in range(1, side // ROWS // ROWS):
        part = jnp.where(group == q, wide[q * ROWS : (q + 1) * ROWS], part)

    def summed(part, box, at, peers, sems, sent):
        box[at] = part

        def copy(slot, d, peer):
            return pltpu.make_async_remote_copy(
                src_ref=box.at[slot],
                dst_ref=box.at[slot],
                send_sem=sent.at[d],
                recv_sem=sems.at[slot],
                device_id=peer,
                device_id_type=MESH,
            )

        n = box.shape[0]
        for d, peer in enumerate(peers):
            copy(at, d, peer).start()
        for d, peer in enumerate(peers):
            copy(lax.rem(at + d + 1, n), d, peer).wait_recv()
        out = box[0]
        for slot in range(1, n):
            out = out + box[slot]
        for d, peer in enumerate(peers):
            copy(at, d, peer).wait_send()
        return out

    part = summed(part, near, near_at, near_peers, near_recv, near_send)
    part = summed(part, far, far_at, far_peers, far_recv, far_send)
    part = summed(part, across, band, band_peers, across_recv, across_send)
    gram[...] = part

    @pl.loop(0, levels)
    def _(level):
        edge_copy(0, level).wait_send()
        edge_copy(1, level).wait_send()
        out_copy(level).wait()


def over_rows(x):
    x = x[0:8] + x[8:16] + (x[16:24] + x[24:32])
    for shift in (4, 2, 1):
        x = x + pltpu.roll(x, shift, 0)
    return jnp.concatenate([x] * 4, axis=0)


def orthonormal(wide_ref, rank):
    size = wide_ref.shape[1]
    lane = lax.broadcasted_iota(jnp.int32, (size, LANES), 1)
    columns = [wide_ref[k] for k in range(rank)]
    narrow = jnp.zeros((size, LANES), jnp.float32)
    for k in range(rank):
        column = columns[k]
        square = over_rows(column * column)
        scaled = column * (1.0 / square)
        for j in range(k + 1, rank):
            columns[j] = columns[j] - scaled * over_rows(column * columns[j])
        unit = column * lax.rsqrt(square)
        wide_ref[k] = unit
        narrow = jnp.where(lane == k, unit, narrow)
    return narrow


def project_kernel(
    rank, gram, pick, stacked, new_basis, cols, weights, wide, gram_wide, out, in_sem, out_sem
):
    slabs, side, width = cols.shape
    levels, fields, _, lat = new_basis.shape[1:]
    size = side // ROWS

    def in_copy(slab):
        return pltpu.make_async_copy(stacked.at[slab], cols.at[slab], in_sem.at[slab])

    def out_copy(slab, slot):
        return pltpu.make_async_copy(
            out.at[slot],
            new_basis.at[:, lax.div(slab, fields), lax.rem(slab, fields)],
            out_sem.at[slot],
        )

    @pl.loop(0, slabs)
    def _(slab):
        in_copy(slab).start()

    packed = gram[...]
    for c in range(size):
        column = jnp.concatenate(
            [
                jnp.broadcast_to(packed[:, q * size + c : q * size + c + 1], (ROWS, LANES))
                for q in range(size // ROWS)
            ],
            axis=0,
        )
        gram_wide[c] = column
        if c < rank:
            wide[c] = column

    def times_gram(narrow):
        parts = [None] * 4
        for c in range(size):
            term = gram_wide[c] * narrow[c : c + 1]
            parts[c % 4] = term if parts[c % 4] is None else parts[c % 4] + term
        return (parts[0] + parts[1]) + (parts[2] + parts[3])

    @pl.loop(0, ITERS - 1)
    def _(sweep):
        block = times_gram(orthonormal(wide, rank))
        for k in range(rank):
            wide[k] = jnp.broadcast_to(block[:, k : k + 1], (size, LANES))

    orthonormal(wide, rank)
    frame = orthonormal(wide, rank)

    across = jnp.dot(frame.T, pick[...], precision=HIGH, preferred_element_type=jnp.float32)
    same = (
        lax.rem(lax.broadcasted_iota(jnp.int32, (ROWS, side), 1), ROWS)
        == lax.broadcasted_iota(jnp.int32, (ROWS, side), 0)
    )
    for k in range(rank):
        rows = jnp.where(same, across[k : k + 1], 0.0)
        high = rows.astype(jnp.bfloat16).astype(jnp.float32)
        weights[0, pl.ds(k * ROWS, ROWS), :] = high
        weights[1, pl.ds(k * ROWS, ROWS), :] = rows - high

    slots = out.shape[0]

    @pl.loop(0, slabs)
    def _(slab):
        slot = lax.rem(slab, slots)

        @pl.when(slab >= slots)
        def _():
            out_copy(slab - slots, slot).wait()

        in_copy(slab).wait()
        both = weights[...].reshape(2 * rank * ROWS, side).astype(jnp.bfloat16)
        found = jnp.dot(both, cols[slab], preferred_element_type=jnp.float32)
        found = found[: rank * ROWS] + found[rank * ROWS :]
        out[slot] = found[:, :lat].reshape(rank, ROWS, lat)
        out_copy(slab, slot).start()

    @pl.loop(slabs - slots, slabs)
    def _(slab):
        out_copy(slab, lax.rem(slab, slots)).wait()


def constants(lat, width, size):
    arc = (np.arange(lat, dtype=np.float32) + np.float32(0.5)) * np.float32(np.pi / lat) - np.float32(np.pi / 2)
    cosine = np.zeros((ROWS, width), np.float32)
    factor = np.zeros((ROWS, width), np.float32)
    cosine[:, :lat] = np.cos(arc.astype(np.float64))
    factor[:, :lat] = np.sqrt(cosine[:, :lat].astype(np.float64)) / (12.0 * cosine[:, :lat].astype(np.float64))
    pick = np.zeros((size * ROWS, LANES), np.float32)
    spread = np.zeros((LANES, size * ROWS), np.float32)
    for c in range(size):
        pick[c * ROWS : (c + 1) * ROWS, c::size] = 1.0
        spread[c, c * ROWS : (c + 1) * ROWS] = 1.0
    return cosine, factor, pick, spread


def on_device(bands, tiles, winds, basis, ground):
    snaps, levels, _, lat = winds.shape[1:]
    rank = basis.shape[0]
    size = rank + snaps
    side = size * ROWS
    width = -(-lat // LANES) * LANES
    near_n, far_n = 8, tiles // 8
    cosine, factor, pick, spread = constants(lat, width, size)
    whole = pl.BlockSpec(memory_space=pltpu.VMEM)
    anywhere = pl.BlockSpec(memory_space=pl.ANY)
    edge = (2, levels, 2 * snaps // 4 * ROWS, lat)
    stacked, gram = pl.pallas_call(
        functools.partial(gather_kernel, bands, tiles, rank, snaps),
        out_shape=(
            jax.ShapeDtypeStruct((2 * levels, side, width), jnp.bfloat16),
            jax.ShapeDtypeStruct((ROWS, LANES), jnp.float32),
        ),
        in_specs=[anywhere, anywhere, whole, whole, whole, whole],
        out_specs=(anywhere, whole),
        scratch_shapes=[
            pltpu.VMEM(winds.shape, jnp.float32),
            pltpu.VMEM(basis.shape, jnp.bfloat16),
            pltpu.VMEM((2 * levels, side, width), jnp.bfloat16),
            pltpu.VMEM(edge, jnp.float32),
            pltpu.VMEM(edge, jnp.float32),
            pltpu.VMEM((ROWS, width), jnp.int32),
            pltpu.VMEM((side, side), jnp.float32),
            pltpu.VMEM((near_n, ROWS, LANES), jnp.float32),
            pltpu.VMEM((far_n, ROWS, LANES), jnp.float32),
            pltpu.VMEM((bands, ROWS, LANES), jnp.float32),
            pltpu.SemaphoreType.DMA((levels,)),
            pltpu.SemaphoreType.DMA((levels,)),
            pltpu.SemaphoreType.DMA((levels,)),
            pltpu.SemaphoreType.DMA((2, levels)),
            pltpu.SemaphoreType.DMA((2, levels)),
            pltpu.SemaphoreType.DMA((near_n,)),
            pltpu.SemaphoreType.DMA((near_n,)),
            pltpu.SemaphoreType.DMA((far_n,)),
            pltpu.SemaphoreType.DMA((far_n,)),
            pltpu.SemaphoreType.DMA((bands,)),
            pltpu.SemaphoreType.DMA((bands,)),
        ],
        compiler_params=pltpu.CompilerParams(collective_id=0, has_side_effects=True),
        name="gather",
    )(winds, basis, ground, jnp.asarray(cosine), jnp.asarray(factor), jnp.asarray(pick))
    return pl.pallas_call(
        functools.partial(project_kernel, rank),
        out_shape=jax.ShapeDtypeStruct(basis.shape, jnp.float32),
        in_specs=[whole, whole, anywhere],
        out_specs=anywhere,
        scratch_shapes=[
            pltpu.VMEM((2 * levels, side, width), jnp.bfloat16),
            pltpu.VMEM((2, rank * ROWS, side), jnp.float32),
            pltpu.VMEM((rank, size, LANES), jnp.float32),
            pltpu.VMEM((size, size, LANES), jnp.float32),
            pltpu.VMEM((4, rank, ROWS, lat), jnp.float32),
            pltpu.SemaphoreType.DMA((2 * levels,)),
            pltpu.SemaphoreType.DMA((4,)),
        ],
        name="project",
    )(gram, jnp.asarray(spread[:size]), stacked)


def solution(mesh):
    return jax.shard_map(
        functools.partial(on_device, mesh.shape["band"], mesh.shape["tile"]),
        mesh=mesh,
        in_specs=(
            P(None, None, "band", "tile", None),
            P(None, "band", None, "tile", None),
            P("tile", None),
        ),
        out_specs=P(None, "band", None, "tile", None),
        check_vma=False,
    )
```

```python
import functools

import jax
import jax.numpy as jnp
import numpy as np
from jax import lax
from jax.experimental import pallas as pl
from jax.experimental.pallas import tpu as pltpu
from jax.sharding import PartitionSpec as P

ITERS = 4
MESH = pl.DeviceIdType.MESH
HIGH = lax.Precision.HIGHEST
LANES = 128
ROWS = 8
SLOTS = 4
GATHER_VMEM = 36 << 20
PROJECT_VMEM = 24 << 20


def padded(x, width):
    return jnp.concatenate([x, jnp.zeros((x.shape[0], width - x.shape[1]), x.dtype)], axis=1)


def turned(x, shift, axis):
    shift %= x.shape[axis]
    return x if shift == 0 else pltpu.roll(x, shift, axis)


def in_pieces(x, count):
    pieces = []
    for _ in range(count):
        piece = x.astype(jnp.bfloat16).astype(jnp.float32)
        pieces.append(piece)
        x = x - piece
    return pieces


def gather_kernel(
    bands, tiles, rank, snaps,
    winds, basis, ground_in, cosine_in, factor_in,
    cols, gram,
    wind, old, send, recv, ground, cosine, factor, keep, total, near, far, across,
    small_sem, wind_sem, old_sem, send_sem, recv_sem, near_send, near_recv, far_send, far_recv, across_send, across_recv,
):
    levels = winds.shape[2]
    lat = winds.shape[4]
    width = cols.shape[2]
    near_n, far_n = near.shape[0], far.shape[0]
    quads = snaps // 4
    band = lax.axis_index("band")
    tile = lax.axis_index("tile")
    right = lax.rem(tile + 1, tiles)
    left = lax.rem(tile + tiles - 1, tiles)

    def wind_copy(level):
        return pltpu.make_async_copy(winds.at[:, :, level], wind.at[:, :, level], wind_sem.at[level])

    def old_copy(level):
        return pltpu.make_async_copy(basis.at[:, level], old.at[:, level], old_sem.at[level])

    def edge_copy(way, level):
        return pltpu.make_async_remote_copy(
            src_ref=send.at[way, level],
            dst_ref=recv.at[way, level],
            send_sem=send_sem.at[way, level],
            recv_sem=recv_sem.at[way, level],
            device_id=(band, right if way == 0 else left),
            device_id_type=MESH,
        )

    near_at = lax.rem(tile, near_n)
    far_at = lax.div(tile, near_n)
    near_peers = [(band, far_at * near_n + lax.rem(near_at + d, near_n)) for d in range(1, near_n)]
    far_peers = [(band, lax.rem(tile + d * near_n, tiles)) for d in range(1, far_n)]
    band_peers = [(lax.rem(band + d, bands), tile) for d in range(1, bands)]
    barrier = pltpu.get_barrier_semaphore()
    greeted = [(band, left), (band, right)] + near_peers + far_peers + band_peers
    for peer in greeted:
        pl.semaphore_signal(barrier, inc=1, device_id=peer, device_id_type=MESH)

    @pl.loop(0, levels)
    def _(level):
        wind_copy(level).start()

    small = [
        pltpu.make_async_copy(source, held, small_sem.at[i])
        for i, (source, held) in enumerate(((ground_in, ground), (cosine_in, cosine), (factor_in, factor)))
    ]
    for copy in small:
        copy.start()

    @pl.loop(0, levels)
    def _(level):
        old_copy(level).start()

    row = lax.broadcasted_iota(jnp.int32, (ROWS, 1), 0)

    lane = lax.broadcasted_iota(jnp.int32, (1, LANES), 1)
    full = lat // LANES
    rest = lat - full * LANES
    groups = 2 * quads

    def pack(level):
        tails = [[], []]
        for field in range(2):
            for quad in range(quads):
                at = [turned(wind[field, 4 * quad + j, level], 2 * j, 0) for j in range(4)]
                at = [[x[:, t * LANES : min((t + 1) * LANES, lat)] for t in range(full + 1)] for x in at]
                for way, order in ((1, (0, 1, 2, 3)), (0, (1, 2, 3, 0))):
                    for t in range(full + 1):
                        a, b, c, d = (at[j][t] for j in order)
                        tile_of = jnp.where(row < 2, a, jnp.where(row < 4, b, jnp.where(row < 6, c, d)))
                        if t < full:
                            slot = ((field * quads + quad) * full + t) * ROWS
                            send[way, level, pl.ds(slot, ROWS), :] = tile_of
                        else:
                            tails[way].append(padded(tile_of, LANES))
        for way in range(2):
            first, second, third, split = tails[way]
            first = jnp.where(lane < rest, first, pltpu.roll(split, rest, 1))
            second = jnp.where(lane < rest, second, pltpu.roll(split, 2 * rest - LANES, 1))
            for t, x in enumerate((first, second, third)):
                send[way, level, pl.ds((groups * full + t) * ROWS, ROWS), :] = x

    def edges_of(way, level):
        found = [
            [recv[way, level, pl.ds((group * full + t) * ROWS, ROWS), :] for t in range(full)] for group in range(groups)
        ]
        first, second, third = (
            recv[way, level, pl.ds((groups * full + t) * ROWS, ROWS), :] for t in range(groups - 1)
        )
        split = jnp.where(
            lane < LANES - rest,
            pltpu.roll(first, LANES - rest, 1),
            pltpu.roll(second, 2 * LANES - 2 * rest, 1),
        )
        return [jnp.concatenate(x + [tail], axis=1) for x, tail in zip(found, (first, second, third, split))]

    wind_copy(0).wait()
    pack(0)
    pl.semaphore_wait(barrier, len(greeted))

    @pl.loop(1, levels)
    def _(level):
        wind_copy(level).wait()
        pack(level)
        edge_copy(0, level - 1).start()
        edge_copy(1, level - 1).start()

    for copy in small:
        copy.wait()
    keep[...] = padded(ground[...], width)
    total[...] = jnp.zeros_like(total)
    edge_copy(0, levels - 1).start()
    edge_copy(1, levels - 1).start()

    @pl.loop(0, levels)
    def _(level):
        old_copy(level).wait()
        for field in range(2):
            for pair in range(rank // 2):
                two = old[pl.ds(2 * pair, 2), level, field].astype(jnp.float32)
                two = two.reshape(2 * ROWS, lat)
                cols[2 * level + field, pl.ds(2 * ROWS * pair, 2 * ROWS), :] = padded(two, width).astype(jnp.bfloat16)

    def along_lon(x, edge, j):
        after = [row == 2 * j, (row == 2 * j) | (row == 2 * j + 1)]
        edge = turned(jnp.where(after[1], edge[0], edge[1]), -2 * j, 0)
        near_diff = turned(jnp.where(row == 0, edge, x), -1, 0) - turned(jnp.where(row == 7, edge, x), 1, 0)
        far_diff = turned(jnp.where(row < 2, edge, x), -2, 0) - turned(jnp.where(row >= 6, edge, x), 2, 0)
        return 8.0 * near_diff - far_diff

    def along_lat(x):
        near_diff = turned(x, -1, 1) - turned(x, 1, 1)
        far_diff = turned(x, -2, 1) - turned(x, 2, 1)
        return 8.0 * near_diff - far_diff

    def product(level):
        out = None
        for field in range(2):
            m = cols[2 * level + field]
            part = lax.dot_general(m, m, (((1,), (1,)), ((), ())), preferred_element_type=jnp.float32)
            out = part if out is None else out + part
        total[...] += out

    def snapshots(level):
        edge_copy(0, level).wait_recv()
        edge_copy(1, level).wait_recv()
        cos = cosine[...]
        scale = jnp.where(band * levels + level < keep[...], factor[...], 0.0)
        arrived = [edges_of(way, level) for way in range(2)]
        for pair in range(snaps // 2):
            found = [[], []]
            for snap in (2 * pair, 2 * pair + 1):
                quad, j = divmod(snap, 4)
                east, north = (padded(wind[field, snap, level], width) for field in range(2))
                edges = [[arrived[way][field * quads + quad] for way in (1, 0)] for field in range(2)]
                found[0].append((along_lon(north, edges[1], j) - along_lat(east * cos)) * scale)
                found[1].append((along_lon(east, edges[0], j) + along_lat(north * cos)) * scale)
            for field in range(2):
                both = jnp.concatenate(found[field], axis=0).astype(jnp.bfloat16)
                cols[2 * level + field, pl.ds((rank + 2 * pair) * ROWS, 2 * ROWS), :] = both

    snapshots(0)

    @pl.loop(1, levels)
    def _(level):
        product(level - 1)
        snapshots(level)

    product(levels - 1)

    side = total.shape[0]
    same = (
        lax.rem(lax.broadcasted_iota(jnp.int32, (ROWS, side), 1), ROWS)
        == lax.broadcasted_iota(jnp.int32, (ROWS, side), 0)
    )
    blocks = jnp.where(same[None], total[...].reshape(side // ROWS, ROWS, side), 0.0).sum(axis=1)
    size = side // ROWS
    pick = lax.div(lax.broadcasted_iota(jnp.int32, (side, LANES), 0), ROWS) == lax.rem(
        lax.broadcasted_iota(jnp.int32, (side, LANES), 1), size
    )
    pieces = in_pieces(blocks, 3)
    wide = jnp.dot(
        jnp.concatenate(pieces, axis=0).astype(jnp.bfloat16),
        pick.astype(jnp.float32).astype(jnp.bfloat16),
        preferred_element_type=jnp.float32,
    )
    wide = wide[:size] + (wide[size : 2 * size] + wide[2 * size :])
    group = lax.div(lax.broadcasted_iota(jnp.int32, (ROWS, LANES), 1), size)
    part = wide[0:ROWS]
    for q in range(1, side // ROWS // ROWS):
        part = jnp.where(group == q, wide[q * ROWS : (q + 1) * ROWS], part)

    def summed(part, box, at, peers, sems, sent):
        box[at] = part

        def copy(slot, d, peer):
            return pltpu.make_async_remote_copy(
                src_ref=box.at[slot],
                dst_ref=box.at[slot],
                send_sem=sent.at[d],
                recv_sem=sems.at[slot],
                device_id=peer,
                device_id_type=MESH,
            )

        n = box.shape[0]
        for d, peer in enumerate(peers):
            copy(at, d, peer).start()
        for d, peer in enumerate(peers):
            copy(lax.rem(at + d + 1, n), d, peer).wait_recv()
        out = box[0]
        for slot in range(1, n):
            out = out + box[slot]
        for d, peer in enumerate(peers):
            copy(at, d, peer).wait_send()
        return out

    part = summed(part, near, near_at, near_peers, near_recv, near_send)
    part = summed(part, far, far_at, far_peers, far_recv, far_send)
    part = summed(part, across, band, band_peers, across_recv, across_send)
    gram[...] = part

    @pl.loop(0, levels)
    def _(level):
        edge_copy(0, level).wait_send()
        edge_copy(1, level).wait_send()


def over_rows(x):
    x = x[0:8] + x[8:16] + (x[16:24] + x[24:32])
    for shift in (4, 2, 1):
        x = x + pltpu.roll(x, shift, 0)
    return jnp.concatenate([x] * 4, axis=0)


def orthonormal(wide_ref, rank):
    size = wide_ref.shape[1]
    lane = lax.broadcasted_iota(jnp.int32, (size, LANES), 1)
    columns = [wide_ref[k] for k in range(rank)]
    narrow = jnp.zeros((size, LANES), jnp.float32)
    for k in range(rank):
        column = columns[k]
        square = over_rows(column * column)
        scaled = column * (1.0 / square)
        for j in range(k + 1, rank):
            columns[j] = columns[j] - scaled * over_rows(column * columns[j])
        unit = column * lax.rsqrt(square)
        wide_ref[k] = unit
        narrow = jnp.where(lane == k, unit, narrow)
    return narrow


def project_kernel(
    rank, gram, cols, new_basis, weights, wide, gram_wide, out, out_sem
):
    slabs, side, width = cols.shape
    levels, fields, _, lat = new_basis.shape[1:]
    size = side // ROWS

    def out_copy(level, slot):
        return pltpu.make_async_copy(out.at[slot], new_basis.at[:, level], out_sem.at[slot])

    packed = gram[...]
    for c in range(size):
        column = jnp.concatenate(
            [
                jnp.broadcast_to(packed[:, q * size + c : q * size + c + 1], (ROWS, LANES))
                for q in range(size // ROWS)
            ],
            axis=0,
        )
        gram_wide[c] = column
        if c < rank:
            wide[c] = column

    def times_gram(narrow):
        parts = [None] * 4
        for c in range(size):
            term = gram_wide[c] * narrow[c : c + 1]
            parts[c % 4] = term if parts[c % 4] is None else parts[c % 4] + term
        return (parts[0] + parts[1]) + (parts[2] + parts[3])

    @pl.loop(0, ITERS - 1)
    def _(sweep):
        block = times_gram(orthonormal(wide, rank))
        for k in range(rank):
            wide[k] = jnp.broadcast_to(block[:, k : k + 1], (size, LANES))

    orthonormal(wide, rank)
    frame = orthonormal(wide, rank)

    spread = lax.broadcasted_iota(jnp.int32, (size, side), 0) == lax.div(
        lax.broadcasted_iota(jnp.int32, (size, side), 1), ROWS
    )
    pieces = [piece.T[:rank] for piece in in_pieces(frame, 2)]
    across = jnp.dot(
        jnp.concatenate(pieces, axis=0).astype(jnp.bfloat16),
        spread.astype(jnp.float32).astype(jnp.bfloat16),
        preferred_element_type=jnp.float32,
    )
    same = (
        lax.rem(lax.broadcasted_iota(jnp.int32, (ROWS, side), 1), ROWS)
        == lax.broadcasted_iota(jnp.int32, (ROWS, side), 0)
    )
    for k in range(rank):
        rows = [jnp.where(same, across[2 * k + i : 2 * k + i + 1], 0.0) for i in range(2)]
        weights[pl.ds(2 * k * ROWS, 2 * ROWS), :] = jnp.concatenate(rows, axis=0).astype(jnp.bfloat16)

    slots = out.shape[0]

    @pl.loop(0, levels)
    def _(level):
        slot = lax.rem(level, slots)

        @pl.when(level >= slots)
        def _():
            out_copy(level - slots, slot).wait()

        for field in range(fields):
            found = jnp.dot(weights[...], cols[fields * level + field], preferred_element_type=jnp.float32)
            found = found[: rank * ROWS] + found[rank * ROWS :]
            out[slot, :, field] = found[:, :lat].reshape(rank, ROWS, lat)
        out_copy(level, slot).start()

    @pl.loop(levels - slots, levels)
    def _(level):
        out_copy(level, lax.rem(level, slots)).wait()


def in_hbm(x):
    return pltpu.with_memory_space_constraint(x, pltpu.HBM)


def constants(lat, width):
    arc = (np.arange(lat, dtype=np.float32) + np.float32(0.5)) * np.float32(np.pi / lat) - np.float32(np.pi / 2)
    cosine = np.zeros((ROWS, width), np.float32)
    factor = np.zeros((ROWS, width), np.float32)
    cosine[:, :lat] = np.cos(arc.astype(np.float64))
    factor[:, :lat] = np.sqrt(cosine[:, :lat].astype(np.float64)) / (12.0 * cosine[:, :lat].astype(np.float64))
    return cosine, factor


def on_device(bands, tiles, winds, basis, ground):
    snaps, levels, _, lat = winds.shape[1:]
    rank = basis.shape[0]
    size = rank + snaps
    side = size * ROWS
    width = -(-lat // LANES) * LANES
    near_n, far_n = 8, tiles // 8
    cosine, factor = constants(lat, width)
    whole = pl.BlockSpec(memory_space=pltpu.VMEM)
    anywhere = pl.BlockSpec(memory_space=pltpu.HBM)
    edge = (2, levels, (snaps // 2 * (lat // LANES) + snaps // 2 - 1) * ROWS, LANES)
    stacked, gram = pl.pallas_call(
        functools.partial(gather_kernel, bands, tiles, rank, snaps),
        out_shape=(
            jax.ShapeDtypeStruct((2 * levels, side, width), jnp.bfloat16),
            jax.ShapeDtypeStruct((ROWS, LANES), jnp.float32),
        ),
        in_specs=[anywhere] * 5,
        out_specs=(whole, whole),
        scratch_shapes=[
            pltpu.VMEM(winds.shape, jnp.float32),
            pltpu.VMEM(basis.shape, jnp.bfloat16),
            pltpu.VMEM(edge, jnp.float32),
            pltpu.VMEM(edge, jnp.float32),
            pltpu.VMEM(ground.shape, jnp.int32),
            pltpu.VMEM((ROWS, width), jnp.float32),
            pltpu.VMEM((ROWS, width), jnp.float32),
            pltpu.VMEM((ROWS, width), jnp.int32),
            pltpu.VMEM((side, side), jnp.float32),
            pltpu.VMEM((near_n, ROWS, LANES), jnp.float32),
            pltpu.VMEM((far_n, ROWS, LANES), jnp.float32),
            pltpu.VMEM((bands, ROWS, LANES), jnp.float32),
            pltpu.SemaphoreType.DMA((3,)),
            pltpu.SemaphoreType.DMA((levels,)),
            pltpu.SemaphoreType.DMA((levels,)),
            pltpu.SemaphoreType.DMA((2, levels)),
            pltpu.SemaphoreType.DMA((2, levels)),
            pltpu.SemaphoreType.DMA((near_n,)),
            pltpu.SemaphoreType.DMA((near_n,)),
            pltpu.SemaphoreType.DMA((far_n,)),
            pltpu.SemaphoreType.DMA((far_n,)),
            pltpu.SemaphoreType.DMA((bands,)),
            pltpu.SemaphoreType.DMA((bands,)),
        ],
        compiler_params=pltpu.CompilerParams(collective_id=0, has_side_effects=True, vmem_limit_bytes=GATHER_VMEM),
        name="gather",
    )(*(in_hbm(x) for x in (winds, basis, ground, jnp.asarray(cosine), jnp.asarray(factor))))
    return pl.pallas_call(
        functools.partial(project_kernel, rank),
        out_shape=jax.ShapeDtypeStruct(basis.shape, jnp.float32),
        in_specs=[whole, whole],
        out_specs=anywhere,
        scratch_shapes=[
            pltpu.VMEM((2 * rank * ROWS, side), jnp.bfloat16),
            pltpu.VMEM((rank, size, LANES), jnp.float32),
            pltpu.VMEM((size, size, LANES), jnp.float32),
            pltpu.VMEM((SLOTS, rank, 2, ROWS, lat), jnp.float32),
            pltpu.SemaphoreType.DMA((SLOTS,)),
        ],
        compiler_params=pltpu.CompilerParams(vmem_limit_bytes=PROJECT_VMEM),
        name="project",
    )(gram, stacked)


def solution(mesh):
    return jax.shard_map(
        functools.partial(on_device, mesh.shape["band"], mesh.shape["tile"]),
        mesh=mesh,
        in_specs=(
            P(None, None, "band", "tile", None),
            P(None, "band", None, "tile", None),
            P("tile", None),
        ),
        out_specs=P(None, "band", None, "tile", None),
        check_vma=False,
    )
```

```python
import functools

import jax
import jax.numpy as jnp
import numpy as np
from jax import lax
from jax.experimental import pallas as pl
from jax.experimental.pallas import tpu as pltpu
from jax.sharding import PartitionSpec as P

ITERS = 4
MESH = pl.DeviceIdType.MESH
LANES = 128
ROWS = 8
SLOTS = 4
GATHER_VMEM = 36 << 20
PROJECT_VMEM = 24 << 20


def padded(x, width):
    return jnp.concatenate([x, jnp.zeros((x.shape[0], width - x.shape[1]), x.dtype)], axis=1)


def turned(x, shift, axis):
    shift %= x.shape[axis]
    return x if shift == 0 else pltpu.roll(x, shift, axis)


def in_pieces(x, count):
    pieces = []
    for _ in range(count):
        piece = x.astype(jnp.bfloat16).astype(jnp.float32)
        pieces.append(piece)
        x = x - piece
    return pieces


def gather_kernel(
    bands, tiles, rank, snaps,
    winds, basis, ground_in, cosine_in, factor_in,
    cols, gram,
    wind, old, send, recv, ground, cosine, factor, keep, total, near, far, across,
    small_sem, wind_sem, old_sem, send_sem, recv_sem, near_send, near_recv, far_send, far_recv, across_send, across_recv,
):
    levels = winds.shape[2]
    lat = winds.shape[4]
    width = cols.shape[2]
    near_n, far_n = near.shape[0], far.shape[0]
    quads = snaps // 4
    band = lax.axis_index("band")
    tile = lax.axis_index("tile")
    right = lax.rem(tile + 1, tiles)
    left = lax.rem(tile + tiles - 1, tiles)

    def wind_copy(level):
        return pltpu.make_async_copy(winds.at[:, :, level], wind.at[:, :, level], wind_sem.at[level])

    def old_copy(level):
        return pltpu.make_async_copy(basis.at[:, level], old.at[:, level], old_sem.at[level])

    def edge_copy(way, level):
        return pltpu.make_async_remote_copy(
            src_ref=send.at[way, level],
            dst_ref=recv.at[way, level],
            send_sem=send_sem.at[way, level],
            recv_sem=recv_sem.at[way, level],
            device_id=(band, right if way == 0 else left),
            device_id_type=MESH,
        )

    wind_copy(0).start()
    near_at = lax.rem(tile, near_n)
    far_at = lax.div(tile, near_n)
    near_peers = [(band, far_at * near_n + lax.rem(near_at + d, near_n)) for d in range(1, near_n)]
    far_peers = [(band, lax.rem(tile + d * near_n, tiles)) for d in range(1, far_n)]
    band_peers = [(lax.rem(band + d, bands), tile) for d in range(1, bands)]
    barrier = pltpu.get_barrier_semaphore()
    greeted = [(band, left), (band, right)] + near_peers + far_peers + band_peers
    for peer in greeted:
        pl.semaphore_signal(barrier, inc=1, device_id=peer, device_id_type=MESH)

    @pl.loop(1, levels)
    def _(level):
        wind_copy(level).start()

    small = [
        pltpu.make_async_copy(source, held, small_sem.at[i])
        for i, (source, held) in enumerate(((ground_in, ground), (cosine_in, cosine), (factor_in, factor)))
    ]
    for copy in small:
        copy.start()

    row = lax.broadcasted_iota(jnp.int32, (ROWS, 1), 0)

    lane = lax.broadcasted_iota(jnp.int32, (1, LANES), 1)
    full = lat // LANES
    rest = lat - full * LANES
    groups = 2 * quads

    def pack(level):
        tails = [[], []]
        for field in range(2):
            for quad in range(quads):
                at = [turned(wind[field, 4 * quad + j, level], 2 * j, 0) for j in range(4)]
                at = [[x[:, t * LANES : min((t + 1) * LANES, lat)] for t in range(full + 1)] for x in at]
                for way, order in ((1, (0, 1, 2, 3)), (0, (1, 2, 3, 0))):
                    for t in range(full + 1):
                        a, b, c, d = (at[j][t] for j in order)
                        tile_of = jnp.where(row < 2, a, jnp.where(row < 4, b, jnp.where(row < 6, c, d)))
                        if t < full:
                            slot = ((field * quads + quad) * full + t) * ROWS
                            send[way, level, pl.ds(slot, ROWS), :] = tile_of
                        else:
                            tails[way].append(padded(tile_of, LANES))
        for way in range(2):
            first, second, third, split = tails[way]
            first = jnp.where(lane < rest, first, pltpu.roll(split, rest, 1))
            second = jnp.where(lane < rest, second, pltpu.roll(split, 2 * rest - LANES, 1))
            for t, x in enumerate((first, second, third)):
                send[way, level, pl.ds((groups * full + t) * ROWS, ROWS), :] = x

    def edges_of(way, level):
        found = [
            [recv[way, level, pl.ds((group * full + t) * ROWS, ROWS), :] for t in range(full)] for group in range(groups)
        ]
        first, second, third = (
            recv[way, level, pl.ds((groups * full + t) * ROWS, ROWS), :] for t in range(groups - 1)
        )
        split = jnp.where(
            lane < LANES - rest,
            pltpu.roll(first, LANES - rest, 1),
            pltpu.roll(second, 2 * LANES - 2 * rest, 1),
        )
        return [jnp.concatenate(x + [tail], axis=1) for x, tail in zip(found, (first, second, third, split))]

    wind_copy(0).wait()
    pack(0)
    pl.semaphore_wait(barrier, len(greeted))

    @pl.loop(1, levels)
    def _(level):
        wind_copy(level).wait()
        pack(level)
        edge_copy(0, level - 1).start()
        edge_copy(1, level - 1).start()
        old_copy(level - 1).start()

    old_copy(levels - 1).start()

    for copy in small:
        copy.wait()
    keep[...] = padded(ground[...], width)
    total[...] = jnp.zeros_like(total)
    edge_copy(0, levels - 1).start()
    edge_copy(1, levels - 1).start()

    @pl.loop(0, levels)
    def _(level):
        old_copy(level).wait()
        for field in range(2):
            for pair in range(rank // 2):
                two = old[pl.ds(2 * pair, 2), level, field].astype(jnp.float32)
                two = two.reshape(2 * ROWS, lat)
                cols[2 * level + field, pl.ds(2 * ROWS * pair, 2 * ROWS), :] = padded(two, width).astype(jnp.bfloat16)

    def along_lon(x, edge, j):
        after = [row == 2 * j, (row == 2 * j) | (row == 2 * j + 1)]
        edge = turned(jnp.where(after[1], edge[0], edge[1]), -2 * j, 0)
        near_diff = turned(jnp.where(row == 0, edge, x), -1, 0) - turned(jnp.where(row == 7, edge, x), 1, 0)
        far_diff = turned(jnp.where(row < 2, edge, x), -2, 0) - turned(jnp.where(row >= 6, edge, x), 2, 0)
        return 8.0 * near_diff - far_diff

    def along_lat(x):
        near_diff = turned(x, -1, 1) - turned(x, 1, 1)
        far_diff = turned(x, -2, 1) - turned(x, 2, 1)
        return 8.0 * near_diff - far_diff

    def product(level):
        out = None
        for field in range(2):
            m = cols[2 * level + field]
            part = lax.dot_general(m, m, (((1,), (1,)), ((), ())), preferred_element_type=jnp.float32)
            out = part if out is None else out + part
        total[...] += out

    def snapshots(level):
        edge_copy(0, level).wait_recv()
        edge_copy(1, level).wait_recv()
        cos = cosine[...]
        scale = jnp.where(band * levels + level < keep[...], factor[...], 0.0)
        arrived = [edges_of(way, level) for way in range(2)]
        for pair in range(snaps // 2):
            found = [[], []]
            for snap in (2 * pair, 2 * pair + 1):
                quad, j = divmod(snap, 4)
                east, north = (padded(wind[field, snap, level], width) for field in range(2))
                edges = [[arrived[way][field * quads + quad] for way in (1, 0)] for field in range(2)]
                found[0].append((along_lon(north, edges[1], j) - along_lat(east * cos)) * scale)
                found[1].append((along_lon(east, edges[0], j) + along_lat(north * cos)) * scale)
            for field in range(2):
                both = jnp.concatenate(found[field], axis=0).astype(jnp.bfloat16)
                cols[2 * level + field, pl.ds((rank + 2 * pair) * ROWS, 2 * ROWS), :] = both

    snapshots(0)

    @pl.loop(1, levels)
    def _(level):
        product(level - 1)
        snapshots(level)

    product(levels - 1)

    side = total.shape[0]
    same = (
        lax.rem(lax.broadcasted_iota(jnp.int32, (ROWS, side), 1), ROWS)
        == lax.broadcasted_iota(jnp.int32, (ROWS, side), 0)
    )
    blocks = jnp.where(same[None], total[...].reshape(side // ROWS, ROWS, side), 0.0).sum(axis=1)
    size = side // ROWS
    pick = lax.div(lax.broadcasted_iota(jnp.int32, (side, LANES), 0), ROWS) == lax.rem(
        lax.broadcasted_iota(jnp.int32, (side, LANES), 1), size
    )
    pieces = in_pieces(blocks, 3)
    wide = jnp.dot(
        jnp.concatenate(pieces, axis=0).astype(jnp.bfloat16),
        pick.astype(jnp.float32).astype(jnp.bfloat16),
        preferred_element_type=jnp.float32,
    )
    wide = wide[:size] + (wide[size : 2 * size] + wide[2 * size :])
    group = lax.div(lax.broadcasted_iota(jnp.int32, (ROWS, LANES), 1), size)
    part = wide[0:ROWS]
    for q in range(1, side // ROWS // ROWS):
        part = jnp.where(group == q, wide[q * ROWS : (q + 1) * ROWS], part)

    def summed(part, box, at, peers, sems, sent):
        box[at] = part

        def copy(slot, d, peer):
            return pltpu.make_async_remote_copy(
                src_ref=box.at[slot],
                dst_ref=box.at[slot],
                send_sem=sent.at[d],
                recv_sem=sems.at[slot],
                device_id=peer,
                device_id_type=MESH,
            )

        n = box.shape[0]
        for d, peer in enumerate(peers):
            copy(at, d, peer).start()
        for d, peer in enumerate(peers):
            copy(lax.rem(at + d + 1, n), d, peer).wait_recv()
        out = box[0]
        for slot in range(1, n):
            out = out + box[slot]
        for d, peer in enumerate(peers):
            copy(at, d, peer).wait_send()
        return out

    part = summed(part, near, near_at, near_peers, near_recv, near_send)
    part = summed(part, far, far_at, far_peers, far_recv, far_send)
    part = summed(part, across, band, band_peers, across_recv, across_send)
    gram[...] = part

    @pl.loop(0, levels)
    def _(level):
        edge_copy(0, level).wait_send()
        edge_copy(1, level).wait_send()


def over_rows(x):
    x = x[0:8] + x[8:16] + (x[16:24] + x[24:32])
    for shift in (4, 2, 1):
        x = x + pltpu.roll(x, shift, 0)
    return jnp.concatenate([x] * 4, axis=0)


def orthonormal(block, rank):
    size = block.shape[0]
    lane = lax.broadcasted_iota(jnp.int32, (size, LANES), 1)
    frame = jnp.zeros((size, LANES), jnp.float32)
    for first in range(0, rank, ROWS):
        ids = range(first, min(first + ROWS, rank))
        columns = {k: jnp.broadcast_to(block[:, k : k + 1], (size, LANES)) for k in ids}
        for k in ids:
            column = columns[k]
            square = over_rows(column * column)
            scaled = column * (1.0 / square)
            for j in ids:
                if j > k:
                    columns[j] = columns[j] - scaled * over_rows(column * columns[j])
            if first + ROWS < rank:
                block = block - scaled * over_rows(column * block)
            frame = jnp.where(lane == k, column * lax.rsqrt(square), frame)
    return frame


def project_kernel(
    rank, gram, cols, new_basis, weights, gram_wide, out, out_sem
):
    slabs, side, width = cols.shape
    levels, fields, _, lat = new_basis.shape[1:]
    size = side // ROWS

    def out_copy(level, slot):
        return pltpu.make_async_copy(out.at[slot], new_basis.at[:, level], out_sem.at[slot])

    packed = gram[...]
    block = jnp.concatenate([turned(packed, -q * size, 1) for q in range(size // ROWS)], axis=0)
    for c in range(size):
        gram_wide[c] = jnp.broadcast_to(block[:, c : c + 1], (size, LANES))

    def times_gram(frame):
        parts = [None] * 4
        for c in range(size):
            term = gram_wide[c] * frame[c : c + 1]
            parts[c % 4] = term if parts[c % 4] is None else parts[c % 4] + term
        return (parts[0] + parts[1]) + (parts[2] + parts[3])

    for sweep in range(ITERS - 1):
        block = times_gram(orthonormal(block, rank))
    frame = orthonormal(orthonormal(block, rank), rank)

    spread = lax.broadcasted_iota(jnp.int32, (size, side), 0) == lax.div(
        lax.broadcasted_iota(jnp.int32, (size, side), 1), ROWS
    )
    pieces = [piece.T[:rank] for piece in in_pieces(frame, 2)]
    across = jnp.dot(
        jnp.concatenate(pieces, axis=0).astype(jnp.bfloat16),
        spread.astype(jnp.float32).astype(jnp.bfloat16),
        preferred_element_type=jnp.float32,
    )
    same = (
        lax.rem(lax.broadcasted_iota(jnp.int32, (ROWS, side), 1), ROWS)
        == lax.broadcasted_iota(jnp.int32, (ROWS, side), 0)
    )
    for k in range(rank):
        rows = [jnp.where(same, across[2 * k + i : 2 * k + i + 1], 0.0) for i in range(2)]
        weights[pl.ds(2 * k * ROWS, 2 * ROWS), :] = jnp.concatenate(rows, axis=0).astype(jnp.bfloat16)

    slots = out.shape[0]

    @pl.loop(0, levels)
    def _(level):
        slot = lax.rem(level, slots)

        @pl.when(level >= slots)
        def _():
            out_copy(level - slots, slot).wait()

        for field in range(fields):
            found = jnp.dot(weights[...], cols[fields * level + field], preferred_element_type=jnp.float32)
            found = found[: rank * ROWS] + found[rank * ROWS :]
            out[slot, :, field] = found[:, :lat].reshape(rank, ROWS, lat)
        out_copy(level, slot).start()

    @pl.loop(levels - slots, levels)
    def _(level):
        out_copy(level, lax.rem(level, slots)).wait()


def in_hbm(x):
    return pltpu.with_memory_space_constraint(x, pltpu.HBM)


def constants(lat, width):
    arc = (np.arange(lat, dtype=np.float32) + np.float32(0.5)) * np.float32(np.pi / lat) - np.float32(np.pi / 2)
    cosine = np.zeros((ROWS, width), np.float32)
    factor = np.zeros((ROWS, width), np.float32)
    cosine[:, :lat] = np.cos(arc.astype(np.float64))
    factor[:, :lat] = np.sqrt(cosine[:, :lat].astype(np.float64)) / (12.0 * cosine[:, :lat].astype(np.float64))
    return cosine, factor


def on_device(bands, tiles, winds, basis, ground):
    snaps, levels, _, lat = winds.shape[1:]
    rank = basis.shape[0]
    size = rank + snaps
    side = size * ROWS
    width = -(-lat // LANES) * LANES
    near_n, far_n = 8, tiles // 8
    cosine, factor = constants(lat, width)
    whole = pl.BlockSpec(memory_space=pltpu.VMEM)
    anywhere = pl.BlockSpec(memory_space=pltpu.HBM)
    edge = (2, levels, (snaps // 2 * (lat // LANES) + snaps // 2 - 1) * ROWS, LANES)
    stacked, gram = pl.pallas_call(
        functools.partial(gather_kernel, bands, tiles, rank, snaps),
        out_shape=(
            jax.ShapeDtypeStruct((2 * levels, side, width), jnp.bfloat16),
            jax.ShapeDtypeStruct((ROWS, LANES), jnp.float32),
        ),
        in_specs=[anywhere] * 5,
        out_specs=(whole, whole),
        scratch_shapes=[
            pltpu.VMEM(winds.shape, jnp.float32),
            pltpu.VMEM(basis.shape, jnp.bfloat16),
            pltpu.VMEM(edge, jnp.float32),
            pltpu.VMEM(edge, jnp.float32),
            pltpu.VMEM(ground.shape, jnp.int32),
            pltpu.VMEM((ROWS, width), jnp.float32),
            pltpu.VMEM((ROWS, width), jnp.float32),
            pltpu.VMEM((ROWS, width), jnp.int32),
            pltpu.VMEM((side, side), jnp.float32),
            pltpu.VMEM((near_n, ROWS, LANES), jnp.float32),
            pltpu.VMEM((far_n, ROWS, LANES), jnp.float32),
            pltpu.VMEM((bands, ROWS, LANES), jnp.float32),
            pltpu.SemaphoreType.DMA((3,)),
            pltpu.SemaphoreType.DMA((levels,)),
            pltpu.SemaphoreType.DMA((levels,)),
            pltpu.SemaphoreType.DMA((2, levels)),
            pltpu.SemaphoreType.DMA((2, levels)),
            pltpu.SemaphoreType.DMA((near_n,)),
            pltpu.SemaphoreType.DMA((near_n,)),
            pltpu.SemaphoreType.DMA((far_n,)),
            pltpu.SemaphoreType.DMA((far_n,)),
            pltpu.SemaphoreType.DMA((bands,)),
            pltpu.SemaphoreType.DMA((bands,)),
        ],
        compiler_params=pltpu.CompilerParams(collective_id=0, has_side_effects=True, vmem_limit_bytes=GATHER_VMEM),
        name="gather",
    )(*(in_hbm(x) for x in (winds, basis, ground, jnp.asarray(cosine), jnp.asarray(factor))))
    return pl.pallas_call(
        functools.partial(project_kernel, rank),
        out_shape=jax.ShapeDtypeStruct(basis.shape, jnp.float32),
        in_specs=[whole, whole],
        out_specs=anywhere,
        scratch_shapes=[
            pltpu.VMEM((2 * rank * ROWS, side), jnp.bfloat16),
            pltpu.VMEM((size, size, LANES), jnp.float32),
            pltpu.VMEM((SLOTS, rank, 2, ROWS, lat), jnp.float32),
            pltpu.SemaphoreType.DMA((SLOTS,)),
        ],
        compiler_params=pltpu.CompilerParams(vmem_limit_bytes=PROJECT_VMEM),
        name="project",
    )(gram, stacked)


def solution(mesh):
    return jax.shard_map(
        functools.partial(on_device, mesh.shape["band"], mesh.shape["tile"]),
        mesh=mesh,
        in_specs=(
            P(None, None, "band", "tile", None),
            P(None, "band", None, "tile", None),
            P("tile", None),
        ),
        out_specs=P(None, "band", None, "tile", None),
        check_vma=False,
    )
```

```python
import functools

import jax
import jax.numpy as jnp
import numpy as np
from jax import lax
from jax.experimental import pallas as pl
from jax.experimental.pallas import tpu as pltpu
from jax.sharding import PartitionSpec as P

ITERS = 4
MESH = pl.DeviceIdType.MESH
LANES = 128
ROWS = 8
SLOTS = 4
GATHER_VMEM = 36 << 20
PROJECT_VMEM = 24 << 20


def padded(x, width):
    return jnp.concatenate([x, jnp.zeros((x.shape[0], width - x.shape[1]), x.dtype)], axis=1)


def turned(x, shift, axis):
    shift %= x.shape[axis]
    return x if shift == 0 else pltpu.roll(x, shift, axis)


def in_pieces(x, count):
    pieces = []
    for _ in range(count):
        piece = x.astype(jnp.bfloat16).astype(jnp.float32)
        pieces.append(piece)
        x = x - piece
    return pieces


def gather_kernel(
    bands, tiles, rank, snaps,
    winds, basis, ground_in, cosine_in, factor_in,
    cols, gram,
    wind, old, send, recv, ground, cosine, factor, keep, total, near, far, across,
    small_sem, wind_sem, old_sem, send_sem, recv_sem, near_send, near_recv, far_send, far_recv, across_send, across_recv,
):
    levels = winds.shape[2]
    lat = winds.shape[4]
    width = cols.shape[2]
    near_n, far_n = near.shape[0], far.shape[0]
    quads = snaps // 4
    band = lax.axis_index("band")
    tile = lax.axis_index("tile")
    right = lax.rem(tile + 1, tiles)
    left = lax.rem(tile + tiles - 1, tiles)

    def wind_copy(level):
        return pltpu.make_async_copy(winds.at[:, :, level], wind.at[:, :, level], wind_sem.at[level])

    def old_copy(level):
        return pltpu.make_async_copy(basis.at[:, level], old.at[:, level], old_sem.at[level])

    lane = lax.broadcasted_iota(jnp.int32, (1, LANES), 1)
    full = lat // LANES
    rest = lat - full * LANES
    half_tiles = (2 * full + 2, 2 * full + 1)

    def edge_slot(quad, field, t):
        return pl.ds((quad * half_tiles[0] + field * full + t) * ROWS, ROWS)

    def edge_copy(way, level, quad):
        rows = pl.ds(quad * half_tiles[0] * ROWS, half_tiles[quad] * ROWS)
        return pltpu.make_async_remote_copy(
            src_ref=send.at[way, level, rows],
            dst_ref=recv.at[way, level, rows],
            send_sem=send_sem.at[way, level, quad],
            recv_sem=recv_sem.at[way, level, quad],
            device_id=(band, right if way == 0 else left),
            device_id_type=MESH,
        )

    wind_copy(0).start()
    near_at = lax.rem(tile, near_n)
    far_at = lax.div(tile, near_n)
    near_peers = [(band, far_at * near_n + lax.rem(near_at + d, near_n)) for d in range(1, near_n)]
    far_peers = [(band, lax.rem(tile + d * near_n, tiles)) for d in range(1, far_n)]
    band_peers = [(lax.rem(band + d, bands), tile) for d in range(1, bands)]
    barrier = pltpu.get_barrier_semaphore()
    greeted = [(band, left), (band, right)] + near_peers + far_peers + band_peers
    for peer in greeted:
        pl.semaphore_signal(barrier, inc=1, device_id=peer, device_id_type=MESH)

    @pl.loop(1, levels)
    def _(level):
        wind_copy(level).start()

    small = [
        pltpu.make_async_copy(source, held, small_sem.at[i])
        for i, (source, held) in enumerate(((ground_in, ground), (cosine_in, cosine), (factor_in, factor)))
    ]
    for copy in small:
        copy.start()

    row = lax.broadcasted_iota(jnp.int32, (ROWS, 1), 0)

    def pack(level):
        tails = [[], []]
        for quad in range(quads):
            for field in range(2):
                at = [turned(wind[field, 4 * quad + j, level], 2 * j, 0) for j in range(4)]
                at = [[x[:, t * LANES : min((t + 1) * LANES, lat)] for t in range(full + 1)] for x in at]
                for way, order in ((1, (0, 1, 2, 3)), (0, (1, 2, 3, 0))):
                    for t in range(full + 1):
                        a, b, c, d = (at[j][t] for j in order)
                        tile_of = jnp.where(row < 2, a, jnp.where(row < 4, b, jnp.where(row < 6, c, d)))
                        if t < full:
                            send[way, level, edge_slot(quad, field, t), :] = tile_of
                        else:
                            tails[way].append(padded(tile_of, LANES))
        for way in range(2):
            first, second, third, split = tails[way]
            first = jnp.where(lane < rest, first, pltpu.roll(split, rest, 1))
            second = jnp.where(lane < rest, second, pltpu.roll(split, 2 * rest - LANES, 1))
            send[way, level, edge_slot(0, 2, 0), :] = first
            send[way, level, edge_slot(0, 2, 1), :] = second
            send[way, level, edge_slot(1, 2, 0), :] = third

    def edges_of(way, level, quad):
        found = [[recv[way, level, edge_slot(quad, field, t), :] for t in range(full)] for field in range(2)]
        first, second = (recv[way, level, edge_slot(0, 2, t), :] for t in range(2))
        if quad:
            third = recv[way, level, edge_slot(1, 2, 0), :]
            split = jnp.where(
                lane < LANES - rest,
                pltpu.roll(first, LANES - rest, 1),
                pltpu.roll(second, 2 * LANES - 2 * rest, 1),
            )
            first, second = third, split
        return [jnp.concatenate(x + [tail], axis=1) for x, tail in zip(found, (first, second))]

    def all_edges(level):
        return [edge_copy(way, level, quad) for quad in range(quads) for way in range(2)]

    wind_copy(0).wait()
    pack(0)
    pl.semaphore_wait(barrier, len(greeted))

    @pl.loop(1, levels)
    def _(level):
        wind_copy(level).wait()
        pack(level)
        for copy in all_edges(level - 1):
            copy.start()
        old_copy(level - 1).start()

    old_copy(levels - 1).start()

    for copy in small:
        copy.wait()
    keep[...] = padded(ground[...], width)
    total[...] = jnp.zeros_like(total)
    for copy in all_edges(levels - 1):
        copy.start()

    @pl.loop(0, levels)
    def _(level):
        old_copy(level).wait()
        for field in range(2):
            for pair in range(rank // 2):
                two = old[pl.ds(2 * pair, 2), level, field].astype(jnp.float32)
                two = two.reshape(2 * ROWS, lat)
                cols[2 * level + field, pl.ds(2 * ROWS * pair, 2 * ROWS), :] = padded(two, width).astype(jnp.bfloat16)

    def along_lon(x, edge, j):
        after = [row == 2 * j, (row == 2 * j) | (row == 2 * j + 1)]
        edge = turned(jnp.where(after[1], edge[0], edge[1]), -2 * j, 0)
        near_diff = turned(jnp.where(row == 0, edge, x), -1, 0) - turned(jnp.where(row == 7, edge, x), 1, 0)
        far_diff = turned(jnp.where(row < 2, edge, x), -2, 0) - turned(jnp.where(row >= 6, edge, x), 2, 0)
        return 8.0 * near_diff - far_diff

    def along_lat(x):
        near_diff = turned(x, -1, 1) - turned(x, 1, 1)
        far_diff = turned(x, -2, 1) - turned(x, 2, 1)
        return 8.0 * near_diff - far_diff

    def product(level):
        out = None
        for field in range(2):
            m = cols[2 * level + field]
            part = lax.dot_general(m, m, (((1,), (1,)), ((), ())), preferred_element_type=jnp.float32)
            out = part if out is None else out + part
        total[...] += out

    def snapshots(level):
        cos = cosine[...]
        scale = jnp.where(band * levels + level < keep[...], factor[...], 0.0)
        for pair in range(snaps // 2):
            if pair % 2 == 0:
                for way in range(2):
                    edge_copy(way, level, pair // 2).wait_recv()
                arrived = [edges_of(way, level, pair // 2) for way in range(2)]
            found = [[], []]
            for snap in (2 * pair, 2 * pair + 1):
                quad, j = divmod(snap, 4)
                east, north = (padded(wind[field, snap, level], width) for field in range(2))
                edges = [[arrived[way][field] for way in (1, 0)] for field in range(2)]
                found[0].append((along_lon(north, edges[1], j) - along_lat(east * cos)) * scale)
                found[1].append((along_lon(east, edges[0], j) + along_lat(north * cos)) * scale)
            for field in range(2):
                both = jnp.concatenate(found[field], axis=0).astype(jnp.bfloat16)
                cols[2 * level + field, pl.ds((rank + 2 * pair) * ROWS, 2 * ROWS), :] = both

    snapshots(0)

    @pl.loop(1, levels)
    def _(level):
        product(level - 1)
        snapshots(level)

    product(levels - 1)

    side = total.shape[0]
    same = (
        lax.rem(lax.broadcasted_iota(jnp.int32, (ROWS, side), 1), ROWS)
        == lax.broadcasted_iota(jnp.int32, (ROWS, side), 0)
    )
    blocks = jnp.where(same[None], total[...].reshape(side // ROWS, ROWS, side), 0.0).sum(axis=1)
    size = side // ROWS
    pick = lax.div(lax.broadcasted_iota(jnp.int32, (side, LANES), 0), ROWS) == lax.rem(
        lax.broadcasted_iota(jnp.int32, (side, LANES), 1), size
    )
    pieces = in_pieces(blocks, 3)
    wide = jnp.dot(
        jnp.concatenate(pieces, axis=0).astype(jnp.bfloat16),
        pick.astype(jnp.float32).astype(jnp.bfloat16),
        preferred_element_type=jnp.float32,
    )
    wide = wide[:size] + (wide[size : 2 * size] + wide[2 * size :])
    group = lax.div(lax.broadcasted_iota(jnp.int32, (ROWS, LANES), 1), size)
    part = wide[0:ROWS]
    for q in range(1, side // ROWS // ROWS):
        part = jnp.where(group == q, wide[q * ROWS : (q + 1) * ROWS], part)

    def summed(part, box, at, peers, sems, sent):
        box[at] = part

        def copy(slot, d, peer):
            return pltpu.make_async_remote_copy(
                src_ref=box.at[slot],
                dst_ref=box.at[slot],
                send_sem=sent.at[d],
                recv_sem=sems.at[slot],
                device_id=peer,
                device_id_type=MESH,
            )

        n = box.shape[0]
        for d, peer in enumerate(peers):
            copy(at, d, peer).start()
        for d, peer in enumerate(peers):
            copy(lax.rem(at + d + 1, n), d, peer).wait_recv()
        out = box[0]
        for slot in range(1, n):
            out = out + box[slot]
        for d, peer in enumerate(peers):
            copy(at, d, peer).wait_send()
        return out

    part = summed(part, near, near_at, near_peers, near_recv, near_send)
    part = summed(part, far, far_at, far_peers, far_recv, far_send)
    part = summed(part, across, band, band_peers, across_recv, across_send)
    gram[...] = part

    @pl.loop(0, levels)
    def _(level):
        for copy in all_edges(level):
            copy.wait_send()


def over_rows(x):
    x = x[0:8] + x[8:16] + (x[16:24] + x[24:32])
    for shift in (4, 2, 1):
        x = x + pltpu.roll(x, shift, 0)
    return jnp.concatenate([x] * 4, axis=0)


def orthonormal(block, rank):
    size = block.shape[0]
    lane = lax.broadcasted_iota(jnp.int32, (size, LANES), 1)
    frame = jnp.zeros((size, LANES), jnp.float32)
    for first in range(0, rank, ROWS):
        ids = range(first, min(first + ROWS, rank))
        columns = {k: jnp.broadcast_to(block[:, k : k + 1], (size, LANES)) for k in ids}
        for k in ids:
            column = columns[k]
            square = over_rows(column * column)
            scaled = column * (1.0 / square)
            for j in ids:
                if j > k:
                    columns[j] = columns[j] - scaled * over_rows(column * columns[j])
            if first + ROWS < rank:
                block = block - scaled * over_rows(column * block)
            frame = jnp.where(lane == k, column * lax.rsqrt(square), frame)
    return frame


def project_kernel(
    rank, gram, cols, new_basis, weights, gram_wide, out, out_sem
):
    slabs, side, width = cols.shape
    levels, fields, _, lat = new_basis.shape[1:]
    size = side // ROWS

    def out_copy(level, slot, field):
        return pltpu.make_async_copy(
            out.at[slot, :, field], new_basis.at[:, level, field], out_sem.at[slot, field]
        )

    packed = gram[...]
    block = jnp.concatenate([turned(packed, -q * size, 1) for q in range(size // ROWS)], axis=0)
    for c in range(size):
        gram_wide[c] = jnp.broadcast_to(block[:, c : c + 1], (size, LANES))

    def times_gram(frame):
        parts = [None] * 4
        for c in range(size):
            term = gram_wide[c] * frame[c : c + 1]
            parts[c % 4] = term if parts[c % 4] is None else parts[c % 4] + term
        return (parts[0] + parts[1]) + (parts[2] + parts[3])

    for sweep in range(ITERS - 1):
        block = times_gram(orthonormal(block, rank))
    frame = orthonormal(orthonormal(block, rank), rank)

    spread = lax.broadcasted_iota(jnp.int32, (size, side), 0) == lax.div(
        lax.broadcasted_iota(jnp.int32, (size, side), 1), ROWS
    )
    pieces = [piece.T[:rank] for piece in in_pieces(frame, 2)]
    across = jnp.dot(
        jnp.concatenate(pieces, axis=0).astype(jnp.bfloat16),
        spread.astype(jnp.float32).astype(jnp.bfloat16),
        preferred_element_type=jnp.float32,
    )
    same = (
        lax.rem(lax.broadcasted_iota(jnp.int32, (ROWS, side), 1), ROWS)
        == lax.broadcasted_iota(jnp.int32, (ROWS, side), 0)
    )
    for k in range(rank):
        rows = [jnp.where(same, across[2 * k + i : 2 * k + i + 1], 0.0) for i in range(2)]
        weights[pl.ds(2 * k * ROWS, 2 * ROWS), :] = jnp.concatenate(rows, axis=0).astype(jnp.bfloat16)

    slots = out.shape[0]

    @pl.loop(0, levels)
    def _(level):
        slot = lax.rem(level, slots)

        @pl.when(level >= slots)
        def _():
            for field in range(fields):
                out_copy(level - slots, slot, field).wait()

        for field in range(fields):
            found = jnp.dot(weights[...], cols[fields * level + field], preferred_element_type=jnp.float32)
            found = found[: rank * ROWS] + found[rank * ROWS :]
            out[slot, :, field] = found[:, :lat].reshape(rank, ROWS, lat)
            out_copy(level, slot, field).start()

    @pl.loop(levels - slots, levels)
    def _(level):
        for field in range(fields):
            out_copy(level, lax.rem(level, slots), field).wait()


def in_hbm(x):
    return pltpu.with_memory_space_constraint(x, pltpu.HBM)


def constants(lat, width):
    arc = (np.arange(lat, dtype=np.float32) + np.float32(0.5)) * np.float32(np.pi / lat) - np.float32(np.pi / 2)
    cosine = np.zeros((ROWS, width), np.float32)
    factor = np.zeros((ROWS, width), np.float32)
    cosine[:, :lat] = np.cos(arc.astype(np.float64))
    factor[:, :lat] = np.sqrt(cosine[:, :lat].astype(np.float64)) / (12.0 * cosine[:, :lat].astype(np.float64))
    return cosine, factor


def on_device(bands, tiles, winds, basis, ground):
    snaps, levels, _, lat = winds.shape[1:]
    rank = basis.shape[0]
    size = rank + snaps
    side = size * ROWS
    width = -(-lat // LANES) * LANES
    near_n, far_n = 8, tiles // 8
    cosine, factor = constants(lat, width)
    whole = pl.BlockSpec(memory_space=pltpu.VMEM)
    anywhere = pl.BlockSpec(memory_space=pltpu.HBM)
    edge = (2, levels, (snaps // 2 * (lat // LANES) + snaps // 2 - 1) * ROWS, LANES)
    stacked, gram = pl.pallas_call(
        functools.partial(gather_kernel, bands, tiles, rank, snaps),
        out_shape=(
            jax.ShapeDtypeStruct((2 * levels, side, width), jnp.bfloat16),
            jax.ShapeDtypeStruct((ROWS, LANES), jnp.float32),
        ),
        in_specs=[anywhere] * 5,
        out_specs=(whole, whole),
        scratch_shapes=[
            pltpu.VMEM(winds.shape, jnp.float32),
            pltpu.VMEM(basis.shape, jnp.bfloat16),
            pltpu.VMEM(edge, jnp.float32),
            pltpu.VMEM(edge, jnp.float32),
            pltpu.VMEM(ground.shape, jnp.int32),
            pltpu.VMEM((ROWS, width), jnp.float32),
            pltpu.VMEM((ROWS, width), jnp.float32),
            pltpu.VMEM((ROWS, width), jnp.int32),
            pltpu.VMEM((side, side), jnp.float32),
            pltpu.VMEM((near_n, ROWS, LANES), jnp.float32),
            pltpu.VMEM((far_n, ROWS, LANES), jnp.float32),
            pltpu.VMEM((bands, ROWS, LANES), jnp.float32),
            pltpu.SemaphoreType.DMA((3,)),
            pltpu.SemaphoreType.DMA((levels,)),
            pltpu.SemaphoreType.DMA((levels,)),
            pltpu.SemaphoreType.DMA((2, levels, 2)),
            pltpu.SemaphoreType.DMA((2, levels, 2)),
            pltpu.SemaphoreType.DMA((near_n,)),
            pltpu.SemaphoreType.DMA((near_n,)),
            pltpu.SemaphoreType.DMA((far_n,)),
            pltpu.SemaphoreType.DMA((far_n,)),
            pltpu.SemaphoreType.DMA((bands,)),
            pltpu.SemaphoreType.DMA((bands,)),
        ],
        compiler_params=pltpu.CompilerParams(collective_id=0, has_side_effects=True, vmem_limit_bytes=GATHER_VMEM),
        name="gather",
    )(*(in_hbm(x) for x in (winds, basis, ground, jnp.asarray(cosine), jnp.asarray(factor))))
    return pl.pallas_call(
        functools.partial(project_kernel, rank),
        out_shape=jax.ShapeDtypeStruct(basis.shape, jnp.float32),
        in_specs=[whole, whole],
        out_specs=anywhere,
        scratch_shapes=[
            pltpu.VMEM((2 * rank * ROWS, side), jnp.bfloat16),
            pltpu.VMEM((size, size, LANES), jnp.float32),
            pltpu.VMEM((SLOTS, rank, 2, ROWS, lat), jnp.float32),
            pltpu.SemaphoreType.DMA((SLOTS, 2)),
        ],
        compiler_params=pltpu.CompilerParams(vmem_limit_bytes=PROJECT_VMEM),
        name="project",
    )(gram, stacked)


def solution(mesh):
    return jax.shard_map(
        functools.partial(on_device, mesh.shape["band"], mesh.shape["tile"]),
        mesh=mesh,
        in_specs=(
            P(None, None, "band", "tile", None),
            P(None, "band", None, "tile", None),
            P("tile", None),
        ),
        out_specs=P(None, "band", None, "tile", None),
        check_vma=False,
    )
```

```python
import functools

import jax
import jax.numpy as jnp
import numpy as np
from jax import lax
from jax.experimental import pallas as pl
from jax.experimental.pallas import tpu as pltpu
from jax.sharding import PartitionSpec as P

ITERS = 4
MESH = pl.DeviceIdType.MESH
LANES = 128
ROWS = 8
SLOTS = 4
GATHER_VMEM = 36 << 20
PROJECT_VMEM = 24 << 20


def padded(x, width):
    return jnp.concatenate([x, jnp.zeros((x.shape[0], width - x.shape[1]), x.dtype)], axis=1)


def turned(x, shift, axis):
    shift %= x.shape[axis]
    return x if shift == 0 else pltpu.roll(x, shift, axis)


def in_pieces(x, count):
    pieces = []
    for _ in range(count):
        piece = x.astype(jnp.bfloat16).astype(jnp.float32)
        pieces.append(piece)
        x = x - piece
    return pieces


def gather_kernel(
    bands, tiles, rank, snaps,
    winds, basis, ground_in, cosine_in, factor_in,
    cols, gram,
    wind, old, send, recv, ground, cosine, factor, keep, total, near, far,
    small_sem, wind_sem, old_sem, send_sem, recv_sem, near_send, near_recv, far_send, far_recv,
):
    levels = winds.shape[2]
    lat = winds.shape[4]
    width = cols.shape[2]
    near_n = near.shape[0]
    quads = snaps // 4
    band = lax.axis_index("band")
    tile = lax.axis_index("tile")
    right = lax.rem(tile + 1, tiles)
    left = lax.rem(tile + tiles - 1, tiles)

    def wind_copy(level):
        return pltpu.make_async_copy(winds.at[:, :, level], wind.at[:, :, level], wind_sem.at[level])

    def old_copy(level):
        return pltpu.make_async_copy(basis.at[:, level], old.at[:, level], old_sem.at[level])

    def edge_copy(way, level):
        return pltpu.make_async_remote_copy(
            src_ref=send.at[way, level],
            dst_ref=recv.at[way, level],
            send_sem=send_sem.at[way, level],
            recv_sem=recv_sem.at[way, level],
            device_id=(band, right if way == 0 else left),
            device_id_type=MESH,
        )

    wind_copy(0).start()
    near_at = lax.rem(tile, near_n)
    far_at = lax.div(tile, near_n)
    near_peers = [
        (lax.rem(near_at + d, near_n), (band, far_at * near_n + lax.rem(near_at + d, near_n)))
        for d in sorted(range(1, near_n), key=lambda d: abs(d - near_n // 2))
    ]
    wide_n = tiles // near_n
    apart = [(dy, dx) for dy in range(bands) for dx in range(wide_n) if dy or dx]
    apart.sort(key=lambda at: -(min(at[0], bands - at[0]) + min(at[1], wide_n - at[1])))
    far_peers = [
        (
            lax.rem(band + dy, bands) * wide_n + lax.rem(far_at + dx, wide_n),
            (lax.rem(band + dy, bands), lax.rem(tile + dx * near_n, tiles)),
        )
        for dy, dx in apart
    ]
    barrier = pltpu.get_barrier_semaphore()
    greeted = [(band, left), (band, right)] + [peer for _, peer in near_peers + far_peers]
    for peer in greeted:
        pl.semaphore_signal(barrier, inc=1, device_id=peer, device_id_type=MESH)

    @pl.loop(1, levels)
    def _(level):
        wind_copy(level).start()

    small = [
        pltpu.make_async_copy(source, held, small_sem.at[i])
        for i, (source, held) in enumerate(((ground_in, ground), (cosine_in, cosine), (factor_in, factor)))
    ]
    for copy in small:
        copy.start()

    row = lax.broadcasted_iota(jnp.int32, (ROWS, 1), 0)

    lane = lax.broadcasted_iota(jnp.int32, (1, LANES), 1)
    full = lat // LANES
    rest = lat - full * LANES
    groups = 2 * quads

    def pack(level):
        tails = [[], []]
        for field in range(2):
            for quad in range(quads):
                at = [turned(wind[field, 4 * quad + j, level], 2 * j, 0) for j in range(4)]
                at = [[x[:, t * LANES : min((t + 1) * LANES, lat)] for t in range(full + 1)] for x in at]
                for way, order in ((1, (0, 1, 2, 3)), (0, (1, 2, 3, 0))):
                    for t in range(full + 1):
                        a, b, c, d = (at[j][t] for j in order)
                        tile_of = jnp.where(row < 2, a, jnp.where(row < 4, b, jnp.where(row < 6, c, d)))
                        if t < full:
                            slot = ((field * quads + quad) * full + t) * ROWS
                            send[way, level, pl.ds(slot, ROWS), :] = tile_of
                        else:
                            tails[way].append(padded(tile_of, LANES))
        for way in range(2):
            first, second, third, split = tails[way]
            first = jnp.where(lane < rest, first, pltpu.roll(split, rest, 1))
            second = jnp.where(lane < rest, second, pltpu.roll(split, 2 * rest - LANES, 1))
            for t, x in enumerate((first, second, third)):
                send[way, level, pl.ds((groups * full + t) * ROWS, ROWS), :] = x

    def edges_of(way, level):
        found = [
            [recv[way, level, pl.ds((group * full + t) * ROWS, ROWS), :] for t in range(full)] for group in range(groups)
        ]
        first, second, third = (
            recv[way, level, pl.ds((groups * full + t) * ROWS, ROWS), :] for t in range(groups - 1)
        )
        split = jnp.where(
            lane < LANES - rest,
            pltpu.roll(first, LANES - rest, 1),
            pltpu.roll(second, 2 * LANES - 2 * rest, 1),
        )
        return [jnp.concatenate(x + [tail], axis=1) for x, tail in zip(found, (first, second, third, split))]

    wind_copy(0).wait()
    pack(0)
    pl.semaphore_wait(barrier, len(greeted))

    @pl.loop(1, levels)
    def _(level):
        wind_copy(level).wait()
        pack(level)
        edge_copy(0, level - 1).start()
        edge_copy(1, level - 1).start()
        old_copy(level - 1).start()

    old_copy(levels - 1).start()

    for copy in small:
        copy.wait()
    keep[...] = padded(ground[...], width)
    total[...] = jnp.zeros_like(total)
    edge_copy(0, levels - 1).start()
    edge_copy(1, levels - 1).start()

    @pl.loop(0, levels)
    def _(level):
        old_copy(level).wait()
        for field in range(2):
            for pair in range(rank // 2):
                two = old[pl.ds(2 * pair, 2), level, field].astype(jnp.float32)
                two = two.reshape(2 * ROWS, lat)
                cols[2 * level + field, pl.ds(2 * ROWS * pair, 2 * ROWS), :] = padded(two, width).astype(jnp.bfloat16)

    def along_lon(x, edge, j):
        after = [row == 2 * j, (row == 2 * j) | (row == 2 * j + 1)]
        edge = turned(jnp.where(after[1], edge[0], edge[1]), -2 * j, 0)
        near_diff = turned(jnp.where(row == 0, edge, x), -1, 0) - turned(jnp.where(row == 7, edge, x), 1, 0)
        far_diff = turned(jnp.where(row < 2, edge, x), -2, 0) - turned(jnp.where(row >= 6, edge, x), 2, 0)
        return 8.0 * near_diff - far_diff

    def along_lat(x):
        near_diff = turned(x, -1, 1) - turned(x, 1, 1)
        far_diff = turned(x, -2, 1) - turned(x, 2, 1)
        return 8.0 * near_diff - far_diff

    def product(level):
        out = None
        for field in range(2):
            m = cols[2 * level + field]
            part = lax.dot_general(m, m, (((1,), (1,)), ((), ())), preferred_element_type=jnp.float32)
            out = part if out is None else out + part
        total[...] += out

    def snapshots(level):
        edge_copy(0, level).wait_recv()
        edge_copy(1, level).wait_recv()
        cos = cosine[...]
        scale = jnp.where(band * levels + level < keep[...], factor[...], 0.0)
        arrived = [edges_of(way, level) for way in range(2)]
        for pair in range(snaps // 2):
            found = [[], []]
            for snap in (2 * pair, 2 * pair + 1):
                quad, j = divmod(snap, 4)
                east, north = (padded(wind[field, snap, level], width) for field in range(2))
                edges = [[arrived[way][field * quads + quad] for way in (1, 0)] for field in range(2)]
                found[0].append((along_lon(north, edges[1], j) - along_lat(east * cos)) * scale)
                found[1].append((along_lon(east, edges[0], j) + along_lat(north * cos)) * scale)
            for field in range(2):
                both = jnp.concatenate(found[field], axis=0).astype(jnp.bfloat16)
                cols[2 * level + field, pl.ds((rank + 2 * pair) * ROWS, 2 * ROWS), :] = both

    snapshots(0)

    @pl.loop(1, levels)
    def _(level):
        product(level - 1)
        snapshots(level)

    product(levels - 1)

    side = total.shape[0]
    same = (
        lax.rem(lax.broadcasted_iota(jnp.int32, (ROWS, side), 1), ROWS)
        == lax.broadcasted_iota(jnp.int32, (ROWS, side), 0)
    )
    blocks = jnp.where(same[None], total[...].reshape(side // ROWS, ROWS, side), 0.0).sum(axis=1)
    size = side // ROWS
    pick = lax.div(lax.broadcasted_iota(jnp.int32, (side, LANES), 0), ROWS) == lax.rem(
        lax.broadcasted_iota(jnp.int32, (side, LANES), 1), size
    )
    pieces = in_pieces(blocks, 3)
    wide = jnp.dot(
        jnp.concatenate(pieces, axis=0).astype(jnp.bfloat16),
        pick.astype(jnp.float32).astype(jnp.bfloat16),
        preferred_element_type=jnp.float32,
    )
    wide = wide[:size] + (wide[size : 2 * size] + wide[2 * size :])
    group = lax.div(lax.broadcasted_iota(jnp.int32, (ROWS, LANES), 1), size)
    part = wide[0:ROWS]
    for q in range(1, side // ROWS // ROWS):
        part = jnp.where(group == q, wide[q * ROWS : (q + 1) * ROWS], part)

    def summed(part, box, at, peers, sems, sent):
        box[at] = part

        def copy(slot, d, peer):
            return pltpu.make_async_remote_copy(
                src_ref=box.at[slot],
                dst_ref=box.at[slot],
                send_sem=sent.at[d],
                recv_sem=sems.at[slot],
                device_id=peer,
                device_id_type=MESH,
            )

        for d, (_, peer) in enumerate(peers):
            copy(at, d, peer).start()
        for d, (slot, peer) in enumerate(peers):
            copy(slot, d, peer).wait_recv()
        out = box[0]
        for slot in range(1, box.shape[0]):
            out = out + box[slot]
        for d, (_, peer) in enumerate(peers):
            copy(at, d, peer).wait_send()
        return out

    part = summed(part, near, near_at, near_peers, near_recv, near_send)
    part = summed(part, far, band * wide_n + far_at, far_peers, far_recv, far_send)
    gram[...] = part

    @pl.loop(0, levels)
    def _(level):
        edge_copy(0, level).wait_send()
        edge_copy(1, level).wait_send()


def over_rows(x):
    x = x[0:8] + x[8:16] + (x[16:24] + x[24:32])
    for shift in (4, 2, 1):
        x = x + pltpu.roll(x, shift, 0)
    return jnp.concatenate([x] * 4, axis=0)


def orthonormal(block, rank):
    size = block.shape[0]
    lane = lax.broadcasted_iota(jnp.int32, (size, LANES), 1)
    frame = jnp.zeros((size, LANES), jnp.float32)
    for first in range(0, rank, ROWS):
        ids = range(first, min(first + ROWS, rank))
        columns = {k: jnp.broadcast_to(block[:, k : k + 1], (size, LANES)) for k in ids}
        for k in ids:
            column = columns[k]
            square = over_rows(column * column)
            scaled = column * (1.0 / square)
            for j in ids:
                if j > k:
                    columns[j] = columns[j] - scaled * over_rows(column * columns[j])
            if first + ROWS < rank:
                block = block - scaled * over_rows(column * block)
            frame = jnp.where(lane == k, column * lax.rsqrt(square), frame)
    return frame


def project_kernel(
    rank, gram, cols, new_basis, weights, gram_wide, out, out_sem
):
    slabs, side, width = cols.shape
    levels, fields, _, lat = new_basis.shape[1:]
    size = side // ROWS

    def out_copy(level, slot):
        return pltpu.make_async_copy(out.at[slot], new_basis.at[:, level], out_sem.at[slot])

    packed = gram[...]
    block = jnp.concatenate([turned(packed, -q * size, 1) for q in range(size // ROWS)], axis=0)
    for c in range(size):
        gram_wide[c] = jnp.broadcast_to(block[:, c : c + 1], (size, LANES))

    def times_gram(frame):
        parts = [None] * 4
        for c in range(size):
            term = gram_wide[c] * frame[c : c + 1]
            parts[c % 4] = term if parts[c % 4] is None else parts[c % 4] + term
        return (parts[0] + parts[1]) + (parts[2] + parts[3])

    for sweep in range(ITERS - 1):
        block = times_gram(orthonormal(block, rank))
    frame = orthonormal(orthonormal(block, rank), rank)

    spread = lax.broadcasted_iota(jnp.int32, (size, side), 0) == lax.div(
        lax.broadcasted_iota(jnp.int32, (size, side), 1), ROWS
    )
    pieces = [piece.T[:rank] for piece in in_pieces(frame, 2)]
    across = jnp.dot(
        jnp.concatenate(pieces, axis=0).astype(jnp.bfloat16),
        spread.astype(jnp.float32).astype(jnp.bfloat16),
        preferred_element_type=jnp.float32,
    )
    same = (
        lax.rem(lax.broadcasted_iota(jnp.int32, (ROWS, side), 1), ROWS)
        == lax.broadcasted_iota(jnp.int32, (ROWS, side), 0)
    )
    for k in range(rank):
        rows = [jnp.where(same, across[2 * k + i : 2 * k + i + 1], 0.0) for i in range(2)]
        weights[pl.ds(2 * k * ROWS, 2 * ROWS), :] = jnp.concatenate(rows, axis=0).astype(jnp.bfloat16)

    slots = out.shape[0]

    @pl.loop(0, levels)
    def _(level):
        slot = lax.rem(level, slots)

        @pl.when(level >= slots)
        def _():
            out_copy(level - slots, slot).wait()

        for field in range(fields):
            found = jnp.dot(weights[...], cols[fields * level + field], preferred_element_type=jnp.float32)
            found = found[: rank * ROWS] + found[rank * ROWS :]
            out[slot, :, field] = found[:, :lat].reshape(rank, ROWS, lat)
        out_copy(level, slot).start()

    @pl.loop(levels - slots, levels)
    def _(level):
        out_copy(level, lax.rem(level, slots)).wait()


def in_hbm(x):
    return pltpu.with_memory_space_constraint(x, pltpu.HBM)


def constants(lat, width):
    arc = (np.arange(lat, dtype=np.float32) + np.float32(0.5)) * np.float32(np.pi / lat) - np.float32(np.pi / 2)
    cosine = np.zeros((ROWS, width), np.float32)
    factor = np.zeros((ROWS, width), np.float32)
    cosine[:, :lat] = np.cos(arc.astype(np.float64))
    factor[:, :lat] = np.sqrt(cosine[:, :lat].astype(np.float64)) / (12.0 * cosine[:, :lat].astype(np.float64))
    return cosine, factor


def on_device(bands, tiles, winds, basis, ground):
    snaps, levels, _, lat = winds.shape[1:]
    rank = basis.shape[0]
    size = rank + snaps
    side = size * ROWS
    width = -(-lat // LANES) * LANES
    near_n = 8
    far_n = bands * (tiles // near_n)
    cosine, factor = constants(lat, width)
    whole = pl.BlockSpec(memory_space=pltpu.VMEM)
    anywhere = pl.BlockSpec(memory_space=pltpu.HBM)
    edge = (2, levels, (snaps // 2 * (lat // LANES) + snaps // 2 - 1) * ROWS, LANES)
    stacked, gram = pl.pallas_call(
        functools.partial(gather_kernel, bands, tiles, rank, snaps),
        out_shape=(
            jax.ShapeDtypeStruct((2 * levels, side, width), jnp.bfloat16),
            jax.ShapeDtypeStruct((ROWS, LANES), jnp.float32),
        ),
        in_specs=[anywhere] * 5,
        out_specs=(whole, whole),
        scratch_shapes=[
            pltpu.VMEM(winds.shape, jnp.float32),
            pltpu.VMEM(basis.shape, jnp.bfloat16),
            pltpu.VMEM(edge, jnp.float32),
            pltpu.VMEM(edge, jnp.float32),
            pltpu.VMEM(ground.shape, jnp.int32),
            pltpu.VMEM((ROWS, width), jnp.float32),
            pltpu.VMEM((ROWS, width), jnp.float32),
            pltpu.VMEM((ROWS, width), jnp.int32),
            pltpu.VMEM((side, side), jnp.float32),
            pltpu.VMEM((near_n, ROWS, LANES), jnp.float32),
            pltpu.VMEM((far_n, ROWS, LANES), jnp.float32),
            pltpu.SemaphoreType.DMA((3,)),
            pltpu.SemaphoreType.DMA((levels,)),
            pltpu.SemaphoreType.DMA((levels,)),
            pltpu.SemaphoreType.DMA((2, levels)),
            pltpu.SemaphoreType.DMA((2, levels)),
            pltpu.SemaphoreType.DMA((near_n,)),
            pltpu.SemaphoreType.DMA((near_n,)),
            pltpu.SemaphoreType.DMA((far_n,)),
            pltpu.SemaphoreType.DMA((far_n,)),
        ],
        compiler_params=pltpu.CompilerParams(collective_id=0, has_side_effects=True, vmem_limit_bytes=GATHER_VMEM),
        name="gather",
    )(*(in_hbm(x) for x in (winds, basis, ground, jnp.asarray(cosine), jnp.asarray(factor))))
    return pl.pallas_call(
        functools.partial(project_kernel, rank),
        out_shape=jax.ShapeDtypeStruct(basis.shape, jnp.float32),
        in_specs=[whole, whole],
        out_specs=anywhere,
        scratch_shapes=[
            pltpu.VMEM((2 * rank * ROWS, side), jnp.bfloat16),
            pltpu.VMEM((size, size, LANES), jnp.float32),
            pltpu.VMEM((SLOTS, rank, 2, ROWS, lat), jnp.float32),
            pltpu.SemaphoreType.DMA((SLOTS,)),
        ],
        compiler_params=pltpu.CompilerParams(vmem_limit_bytes=PROJECT_VMEM),
        name="project",
    )(gram, stacked)


def solution(mesh):
    return jax.shard_map(
        functools.partial(on_device, mesh.shape["band"], mesh.shape["tile"]),
        mesh=mesh,
        in_specs=(
            P(None, None, "band", "tile", None),
            P(None, "band", None, "tile", None),
            P("tile", None),
        ),
        out_specs=P(None, "band", None, "tile", None),
        check_vma=False,
    )
```
